32 devices in a mesh: arc: 4 (over x, core), col: 8 (over z, y).
Axes of the slice: x: 2, y: 2, z: 4, core: 2. Of those that a mesh axis runs over, the one named last changes fastest.
Arguments:
- partials: bfloat16 [2048, 4, 8192], P('arc', None, 'col'), may hold values from -0.0625 to 0.0625
- coef: bfloat16 [2048, 256], P('arc'), may hold values from -0.75 to 0.75
- arc_ids: int32 [2048], replicated, may hold values from 0 to 11, never falling along the last dimension, each value on 1 to 512 neighbouring positions
Outputs:
- normal: float32 [8192, 8192], P('col', 'arc')
The draws below stay inside these ranges and needn't reach their ends.
Inputs may be any that keep to these rules, and one draw needn't show every extreme that they name: `arc_ids`: arc numbers never fall along the epochs; every arc holds 1 to 512 epochs and one holds exactly 512.
All inputs are finite; a program needn't handle non-finite values.
Results may differ from the reference program's by a relative error of at most 0.0024.
The reference program's roundings to bfloat16 on the way (of `filtered`) count: a program that leaves them out, or rounds other values in their place, can miss the bound.
Values may be sent and summed in bfloat16 or wider, within the bound.
No kernel may reach another device: no remote copies, remote signals or barrier semaphores. Data moves between devices by JAX's collectives and lax.ppermute only.
A program may use at most 128 MiB of HBM per device.

```python
import math
import jax
import jax.numpy as jnp
import numpy as np
from jax import lax

M = 8192
CH = 4
BAND = 256
FBLK = 128
EPOCHS = 2048
ARCS = 12
ARC_MOST = 512


def block_scale(rng, shape, split, smallest, largest):
    gain = 1.0
    for position, parts in split:
        draws = jax.random.uniform(jax.random.fold_in(jax.random.fold_in(rng, 6), position), (parts,), jnp.float32, smallest / len(split), largest / len(split))
        gain = gain * jnp.repeat(jnp.exp(draws), shape[position] // parts).reshape((-1,) + (1,) * (len(shape) - 1 - position))
    return gain


def split_up(number_of, total, limit, slope):
    weights = [(1 << 20) // math.isqrt(grade ** slope) + 1 for grade in range(2, number_of + 1)]
    rest, given = total - limit - (number_of - 1), [1] * (number_of - 1)
    while rest > 0:
        candidates = [i for i in range(number_of - 1) if given[i] < limit]
        mass, remaining = sum([weights[i] for i in candidates]), rest
        for i in candidates:
            extra = min(limit - given[i], max(1, remaining * weights[i] // mass), rest)
            given[i] = given[i] + extra
            rest = rest - extra
    return np.array([limit] + given)


def ragged_sizes(stream_key, number_of, total, reach, skew):
    if number_of == 2:
        one = jax.random.randint(stream_key, (), max(1, total - reach), min(reach, total - 1) + 1)
        return jnp.stack([one, total - one])
    sizes = jnp.asarray(split_up(number_of, total, reach, skew), jnp.int32)
    couples = (number_of - 1) // 2
    giver, taker = sizes[1:1 + 2 * couples:2], sizes[2:2 + 2 * couples:2]
    slack = jnp.minimum(giver - 1, reach - taker)
    shifted = jax.random.randint(jax.random.fold_in(stream_key, 1), (couples,), 0, 1 << 20) % (slack + 1)
    sizes = sizes.at[1:1 + 2 * couples:2].set(giver - shifted).at[2:2 + 2 * couples:2].set(taker + shifted)
    return sizes[jax.random.permutation(jax.random.fold_in(stream_key, 2), number_of)]


def bell_draw(stream_key, shape, scale, limit, cuts=(), held_as=jnp.bfloat16):
    drawn = scale * jax.random.normal(stream_key, shape, jnp.float32)
    if cuts:
        drawn = drawn * block_scale(stream_key, shape, cuts, -0.22, 0.18)
    return jnp.clip(drawn, -limit, limit).astype(held_as)


def setup_inputs(seed: int = 0) -> dict:
    arg_keys = jax.random.split(jax.random.key(seed), 4)
    partials = bell_draw(arg_keys[0], (EPOCHS, CH, M), (EPOCHS * CH) ** -0.5, 0.0625, ((0, 4), (2, 8)))
    coef = bell_draw(arg_keys[1], (EPOCHS, BAND), 0.05, 0.75, ((0, 4),))
    arc_ids = jnp.searchsorted(jnp.cumsum(ragged_sizes(arg_keys[2], ARCS, EPOCHS, ARC_MOST, 0)), jnp.arange(EPOCHS), side="right").astype(jnp.int32)
    return dict(partials=partials, coef=coef, arc_ids=arc_ids)


def reference(partials, coef, arc_ids):
    ep_all, channels, width = partials.shape
    band = coef.shape[1]
    flat_rows = partials.reshape(ep_all, channels * width)
    extended = jnp.concatenate([jnp.zeros((band, channels * width), partials.dtype), flat_rows], 0)
    ids_ext = jnp.concatenate([jnp.full((band,), -1, jnp.int32), arc_ids.astype(jnp.int32)])
    span = FBLK + band

    def one_block(block):
        start = (block * FBLK).astype(jnp.int32)
        window = lax.dynamic_slice_in_dim(extended, start, span, 0)
        ids_win = lax.dynamic_slice_in_dim(ids_ext, start, span, 0)
        coef_blk = lax.dynamic_slice_in_dim(coef, start, FBLK, 0)
        row_pos = jnp.arange(FBLK, dtype=jnp.int32)[:, None]
        col_pos = jnp.arange(span, dtype=jnp.int32)[None, :]
        lag = row_pos + band - col_pos
        picked = jnp.take_along_axis(coef_blk, jnp.clip(lag - 1, 0, band - 1).astype(jnp.int32), axis=1)
        ids_row = ids_win[band:]
        same = ids_row[:, None] == ids_win[None, :]
        inside = (lag >= 1) & (lag <= band) & same
        weight = jnp.where(lag == 0, jnp.ones_like(picked), jnp.where(inside, picked, jnp.zeros_like(picked)))
        return jnp.dot(weight, window, preferred_element_type=jnp.float32).astype(jnp.bfloat16)

    filtered = lax.map(one_block, jnp.arange(ep_all // FBLK, dtype=jnp.int32))
    filtered = filtered.reshape(ep_all * channels, width)
    return lax.dot_general(filtered, filtered, (((0,), (0,)), ((), ())), preferred_element_type=jnp.float32)
```

```python
import functools

import jax
import jax.numpy as jnp
from jax import lax
from jax.experimental import pallas as pl
from jax.experimental.pallas import tpu as pltpu
from jax.sharding import PartitionSpec as P

PIECES = 4
AXES = ("arc", "col")
SPOTS = 4


def band_weights(coef, arc_ids, epochs_here):
    band = coef.shape[1]
    span = epochs_here + band
    start = lax.axis_index("arc") * epochs_here
    ids_all = jnp.concatenate([jnp.full((band,), -1, jnp.int32), arc_ids])
    ids_win = lax.dynamic_slice_in_dim(ids_all, start, span, 0)
    ids_row = lax.dynamic_slice_in_dim(arc_ids, start, epochs_here, 0)
    leading = jnp.concatenate([coef[:, ::-1], jnp.ones((epochs_here, 1), coef.dtype)], 1)
    padded = jnp.concatenate([leading, jnp.zeros((epochs_here, span - band), coef.dtype)], 1)
    skewed = padded.reshape(-1)[: epochs_here * span].reshape(epochs_here, span)
    return jnp.where(ids_row[:, None] == ids_win[None, :], skewed, jnp.zeros_like(skewed))


def window_of(partials, band):
    arcs = lax.axis_size("arc")
    behind = lax.ppermute(partials[partials.shape[0] - band :], "arc", [(a, a + 1) for a in range(arcs - 1)])
    return jnp.concatenate([behind, partials], 0)


def gathered_body(partials, coef, arc_ids):
    epochs_here, channels, width = partials.shape
    weight = band_weights(coef, arc_ids, epochs_here)
    window = window_of(partials, coef.shape[1])
    filtered = jnp.einsum("et,tcm->cem", weight, window, preferred_element_type=jnp.float32)
    filtered = filtered.astype(jnp.bfloat16).reshape(channels * epochs_here, width)
    term = lax.dot_general(
        filtered,
        lax.all_gather(filtered, "col", axis=1, tiled=True),
        (((0,), (0,)), ((), ())),
        preferred_element_type=jnp.float32,
    )
    return lax.psum_scatter(term, "arc", scatter_dimension=1, tiled=True)


def product_kernel(spot_ref, mine_left, other_left, *refs):
    sources = 2 * SPOTS - 1
    mine, other, out, acc = refs[:sources], refs[sources : 2 * sources], refs[2 * sources], refs[2 * sources + 1]
    step = pl.program_id(0)
    spot = spot_ref[0]

    @pl.when(step == 0)
    def _():
        acc[...] = jnp.zeros_like(acc)

    def pick(group, plane):
        taken = group[SPOTS - 1 + (0 - plane)][...]
        for z in range(1, SPOTS):
            taken = jnp.where(spot == z, group[SPOTS - 1 + z - plane][...], taken)
        return taken

    for plane in range(SPOTS):
        acc[plane] += jnp.dot(mine_left[...], pick(mine, plane), preferred_element_type=jnp.float32)
        acc[plane] += jnp.dot(other_left[...], pick(other, plane), preferred_element_type=jnp.float32)

    @pl.when(step == pl.num_programs(0) - 1)
    def _():
        out[...] = acc[...].astype(out.dtype)


def products(spot, mine_left, other_left, mine, other):
    rows, depth = mine_left.shape
    part = mine[0].shape[1]
    steps = 4
    left_spec = pl.BlockSpec((rows, depth // steps), lambda i, s: (0, i))
    right_spec = pl.BlockSpec((depth // steps, part), lambda i, s: (i, 0))
    return pl.pallas_call(
        product_kernel,
        out_shape=jax.ShapeDtypeStruct((SPOTS, rows, part), jnp.bfloat16),
        grid_spec=pltpu.PrefetchScalarGridSpec(
            num_scalar_prefetch=1,
            grid=(steps,),
            in_specs=[left_spec] * 2 + [right_spec] * (2 * len(mine)),
            out_specs=pl.BlockSpec((SPOTS, rows, part), lambda i, s: (0, 0, 0)),
            scratch_shapes=[pltpu.VMEM((SPOTS, rows, part), jnp.float32)],
        ),
        compiler_params=pltpu.CompilerParams(vmem_limit_bytes=48 << 20),
        cost_estimate=pl.CostEstimate(
            flops=4 * SPOTS * rows * depth * part,
            bytes_accessed=4 * rows * depth + 28 * depth * part + 2 * SPOTS * rows * part,
            transcendentals=0,
        ),
    )(spot, mine_left, other_left, *mine, *other)


def pairs(arcs, cols, target):
    found = []
    for half in range(arcs // 2):
        for core in range(2):
            for spot in range(cols // 2):
                for side in range(2):
                    place = target(half, core, spot, side)
                    if place is not None:
                        h, k, z, y = place
                        found.append(((2 * half + core) * cols + 2 * spot + side, (2 * h + k) * cols + 2 * z + y))
    return found


def line_body(partials, coef, arc_ids):
    epochs_here, channels, width = partials.shape
    arcs, cols = lax.axis_size("arc"), lax.axis_size("col")
    col = lax.axis_index("col")
    spot, side = col // 2, col % 2
    rows, part = epochs_here * channels, width // PIECES

    def send(value, target):
        return lax.ppermute(value, AXES, pairs(arcs, cols, target))

    weight = band_weights(coef, arc_ids, epochs_here)
    window = window_of(partials, coef.shape[1])
    own = []
    for piece in range(PIECES):
        taken = window[:, :, piece * part : (piece + 1) * part]
        filtered = jnp.einsum("et,tcm->cem", weight, taken, preferred_element_type=jnp.float32)
        own.append(filtered.astype(jnp.bfloat16).reshape(rows, part))
    left = jnp.einsum("et,tcm->mce", weight, window, preferred_element_type=jnp.float32)
    left = left.astype(jnp.bfloat16).reshape(width, rows)

    def hop(value, hops, step):
        def target(h, k, z, y):
            there, origin = z + step, z - step * (hops - 1)
            return (h, k, there, y) if 0 <= there < SPOTS and 0 <= origin < SPOTS else None

        return send(value, target)

    got = {}
    for piece in range(PIECES):
        got[piece, 0, 1] = got[piece, 0, -1] = own[piece]
    for turn in range(PIECES + SPOTS):
        for hops in range(1, SPOTS):
            piece = turn - (hops - 1)
            if 0 <= piece < PIECES:
                for step in (1, -1):
                    got[piece, hops, step] = hop(got[piece, hops - 1, step], hops, step)
    mine_left = send(left, lambda h, k, z, y: (h, k, z, y if k == 0 else 1 - y))
    other_left = send(left, lambda h, k, z, y: (h, 1 - k, z, y if k == 1 else 1 - y))

    near, far = [], []
    for piece in range(PIECES):
        mine = [got[piece, abs(d), 1 if d > 0 else -1] for d in range(1 - SPOTS, SPOTS)]
        other = [send(value, lambda h, k, z, y: (h, 1 - k, z, y)) for value in mine]
        terms = products(spot.reshape(1), mine_left, other_left, mine, other)
        came = lax.all_to_all(terms, "arc", split_axis=0, concat_axis=0, tiled=True)
        sums = came[:2].astype(jnp.float32) + came[2:].astype(jnp.float32)
        near.append(sums[0])
        far.append(send(sums[1].astype(jnp.bfloat16), lambda h, k, z, y: (h, k, z, 1 - y)).astype(jnp.float32))
    even = [jnp.where(side == 0, a, b) for a, b in zip(near, far)]
    odd = [jnp.where(side == 0, b, a) for a, b in zip(near, far)]
    return jnp.concatenate(even + odd, 1)


def solution(mesh):
    fits = mesh.shape["arc"] == SPOTS and mesh.shape["col"] == 2 * SPOTS
    return jax.shard_map(
        line_body if fits else gathered_body,
        mesh=mesh,
        in_specs=(P("arc", None, "col"), P("arc", None), P()),
        out_specs=P("col", "arc"),
        check_vma=False,
    )
```

```python
import functools

import jax
import jax.numpy as jnp
from jax import lax
from jax.experimental import pallas as pl
from jax.experimental.pallas import tpu as pltpu
from jax.sharding import PartitionSpec as P

PARTS = (4, 2, 2)
AXES = ("arc", "col")
SPOTS = 4


def band_weights(coef, arc_ids, epochs_here):
    band = coef.shape[1]
    span = epochs_here + band
    start = lax.axis_index("arc") * epochs_here
    ids_all = jnp.concatenate([jnp.full((band,), -1, jnp.int32), arc_ids])
    ids_win = lax.dynamic_slice_in_dim(ids_all, start, span, 0)
    ids_row = lax.dynamic_slice_in_dim(arc_ids, start, epochs_here, 0)
    leading = jnp.concatenate([coef[:, ::-1], jnp.ones((epochs_here, 1), coef.dtype)], 1)
    padded = jnp.concatenate([leading, jnp.zeros((epochs_here, span - band), coef.dtype)], 1)
    skewed = padded.reshape(-1)[: epochs_here * span].reshape(epochs_here, span)
    return jnp.where(ids_row[:, None] == ids_win[None, :], skewed, jnp.zeros_like(skewed))


def window_of(partials, band):
    arcs = lax.axis_size("arc")
    behind = lax.ppermute(partials[partials.shape[0] - band :], "arc", [(a, a + 1) for a in range(arcs - 1)])
    return jnp.concatenate([behind, partials], 0)


def gathered_body(partials, coef, arc_ids):
    epochs_here, channels, width = partials.shape
    weight = band_weights(coef, arc_ids, epochs_here)
    window = window_of(partials, coef.shape[1])
    filtered = jnp.einsum("et,tcm->cem", weight, window, preferred_element_type=jnp.float32)
    filtered = filtered.astype(jnp.bfloat16).reshape(channels * epochs_here, width)
    term = lax.dot_general(
        filtered,
        lax.all_gather(filtered, "col", axis=1, tiled=True),
        (((0,), (0,)), ((), ())),
        preferred_element_type=jnp.float32,
    )
    return lax.psum_scatter(term, "arc", scatter_dimension=1, tiled=True)


def filter_kernel(weight, taken, straight, turned):
    found = jnp.dot(weight[...], taken[0], preferred_element_type=jnp.float32).astype(jnp.bfloat16)
    straight[...] = found
    turned[...] = found.T


def filter_half(weight, taken):
    channels, lags, width = taken.shape
    count = weight.shape[0]
    return pl.pallas_call(
        filter_kernel,
        out_shape=(
            jax.ShapeDtypeStruct((channels * count, width), jnp.bfloat16),
            jax.ShapeDtypeStruct((width, channels * count), jnp.bfloat16),
        ),
        grid=(channels,),
        in_specs=[
            pl.BlockSpec((count, lags), lambda c: (0, 0)),
            pl.BlockSpec((1, lags, width), lambda c: (c, 0, 0)),
        ],
        out_specs=(pl.BlockSpec((count, width), lambda c: (c, 0)), pl.BlockSpec((width, count), lambda c: (0, c))),
        compiler_params=pltpu.CompilerParams(vmem_limit_bytes=40 << 20),
        cost_estimate=pl.CostEstimate(
            flops=2 * count * lags * width * channels,
            bytes_accessed=2 * channels * width * (lags + 2 * count),
            transcendentals=0,
        ),
    )(weight, taken)


def product_kernel(flags, *refs):
    near, far, right, outs = refs[:4], refs[4:8], refs[8:12], refs[12:-2]
    left, arrived = refs[-2:]

    @pl.when(pl.program_id(0) == 0)
    def _():
        for value, group in ((0, near), (1, far)):

            @pl.when(flags[0] == value)
            def _():
                copies = [pltpu.make_async_copy(ref, left.at[i], arrived.at[i]) for i, ref in enumerate(group)]
                for copy in copies:
                    copy.start()
                for copy in copies:
                    copy.wait()

    total = jnp.dot(left[0], right[0][...], preferred_element_type=jnp.float32)
    for i in range(1, 4):
        total += jnp.dot(left[i], right[i][...], preferred_element_type=jnp.float32)
    if len(outs) == 1:
        outs[0][...] = total
    else:
        first, keep, give = outs
        swap = flags[1] == 1
        keep[...] = jnp.where(swap, total, first[...])
        give[...] = jnp.where(swap, first[...], total).astype(give.dtype)


def products(flags, near, far, right, start=0, part=None, first=None):
    rows, depth = near[0].shape
    width = rows
    part = part or width
    tile = min(256, part)

    def spec(height, value):
        shift = start // tile if value.shape[1] == width else 0
        return pl.BlockSpec((height, tile), lambda i, w: (0, shift + i))

    here = pl.BlockSpec((rows, tile), lambda i, w: (0, i))
    whole = jax.ShapeDtypeStruct((rows, part), jnp.float32)
    return pl.pallas_call(
        product_kernel,
        out_shape=whole if first is None else (whole, jax.ShapeDtypeStruct((rows, part), jnp.bfloat16)),
        grid_spec=pltpu.PrefetchScalarGridSpec(
            num_scalar_prefetch=1,
            grid=(part // tile,),
            in_specs=[pl.BlockSpec(memory_space=pl.ANY)] * 8
            + [spec(depth, value) for value in right]
            + ([] if first is None else [spec(rows, first)]),
            out_specs=here if first is None else (here, here),
            scratch_shapes=[pltpu.VMEM((4, rows, depth), near[0].dtype), pltpu.SemaphoreType.DMA((4,))],
        ),
        compiler_params=pltpu.CompilerParams(vmem_limit_bytes=40 << 20),
        cost_estimate=pl.CostEstimate(
            flops=depth * part,
            bytes_accessed=depth * part,
            transcendentals=0,
        ),
    )(flags, *near, *far, *right, *([] if first is None else [first]))


def pairs(arcs, cols, target):
    found = []
    for half in range(arcs // 2):
        for core in range(2):
            for spot in range(cols // 2):
                for side in range(2):
                    place = target(half, core, spot, side)
                    if place is not None:
                        h, k, z, y = place
                        found.append(((2 * half + core) * cols + 2 * spot + side, (2 * h + k) * cols + 2 * z + y))
    return found


def line_body(partials, coef, arc_ids):
    epochs_here, channels, width = partials.shape
    band = coef.shape[1]
    arcs, cols = lax.axis_size("arc"), lax.axis_size("col")
    arc, col = lax.axis_index("arc"), lax.axis_index("col")
    half, core, spot, side = arc // 2, arc % 2, col // 2, col % 2
    cut = epochs_here - band
    unit = width // sum(PARTS)
    edges = [unit * sum(PARTS[:i]) for i in range(len(PARTS) + 1)]
    middle = width // 2

    def send(value, target):
        return lax.ppermute(value, AXES, pairs(arcs, cols, target))

    def hop(value, hops, step):
        def target(h, k, z, y):
            there, origin = z + step, z - step * (hops - 1)
            return (h, k, there, y) if 0 <= there < SPOTS and 0 <= origin < SPOTS else None

        return send(value, target)

    def cores(value):
        return send(value, lambda h, k, z, y: (h, 1 - k, z, y))

    def sides(value):
        return send(value, lambda h, k, z, y: (h, k, z, 1 - y))

    def halves(value):
        return send(value, lambda h, k, z, y: (1 - h, k, z, y))

    v = {}

    def fence():
        v.update(lax.optimization_barrier(dict(v)))

    ours = core == spot % 2
    flag_one = jnp.stack([jnp.where(ours, 0, 1), jnp.where(spot // 2 == half, 0, 1)]).astype(jnp.int32)
    flag_two = jnp.stack([jnp.where(ours, 1, 0), jnp.where(spot % 2 == half, 0, 1)]).astype(jnp.int32)
    low, even_spot = spot < SPOTS // 2, spot % 2 == 0

    weight = band_weights(coef, arc_ids, epochs_here)
    behind = lax.ppermute(partials[cut:], "arc", [(a, a + 1) for a in range(arcs - 1)])
    here = jnp.swapaxes(partials, 0, 1)
    v["late"], v["late_t"] = filter_half(weight[band:, band:], here)
    v["up1l"], v["down1l"] = hop(v["late"], 1, 1), hop(v["late"], 1, -1)
    v["far_l"] = sides(v["late_t"])
    v["late_o"] = cores(v["late"])
    behind, _ = lax.optimization_barrier((behind, v["late_o"]))
    v["early"], v["early_t"] = filter_half(
        weight[:band, : 2 * band], jnp.concatenate([jnp.swapaxes(behind, 0, 1), here[:, :band]], 1)
    )
    fence()
    v["up1e"], v["down1e"] = hop(v["early"], 1, 1), hop(v["early"], 1, -1)
    v["far_e"] = sides(v["early_t"])
    v["late_to"], v["early_o"] = cores(v["late_t"]), cores(v["early"])
    fence()

    def near():
        return [v["late_t"], v["late_to"], v["early_t"], v["early_to"]]

    def far():
        return [v["far_l"], v["far_lo"], v["far_e"], v["far_eo"]]

    v["up2l"], v["down2l"] = hop(v["up1l"], 2, 1), hop(v["down1l"], 2, -1)
    v["up2e"], v["down2e"] = hop(v["up1e"], 2, 1), hop(v["down1e"], 2, -1)
    v["early_to"], v["far_lo"], v["far_eo"] = cores(v["early_t"]), cores(v["far_l"]), cores(v["far_e"])
    v["own_t"] = products(flag_one, near(), far(), [v["late"], v["late_o"], v["early"], v["early_o"]])
    low_now, _ = lax.optimization_barrier((low, v["far_eo"]))
    v["next_l"], v["next_e"] = jnp.where(low_now, v["down1l"], v["up1l"]), jnp.where(low_now, v["down1e"], v["up1e"])
    v["next_lo"], v["next_eo"] = cores(v["next_l"]), cores(v["next_e"])
    v["next_t"] = products(flag_two, near(), far(), [v["next_l"], v["next_lo"], v["next_e"], v["next_eo"]])
    fence()

    def over(start):
        right = [v["over_l"], v["over_lo"], v["over_e"], v["over_eo"]]
        return products(flag_one, near(), far(), right, start, middle, v["own_t"])

    def chosen(up, down, stay_up, stay_down):
        stay = jnp.where(even_spot, stay_down, stay_up)
        return jnp.where((spot == 0) | (spot == SPOTS - 1), jnp.where(spot == 0, down, up), stay)

    def last(n):
        a, b = edges[n], edges[n + 1]
        e = chosen(v[f"up3{n}"], v[f"down3{n}"], v["up1e"][:, a:b], v["down1e"][:, a:b])
        return products(flag_two, near(), far(), [v["last_l"], v["last_lo"], e, cores(e)], a, b - a, v["next_t"])

    def third(n):
        v[f"up3{n}"], v[f"down3{n}"] = hop(v[f"up3{n}"], 3, 1), hop(v[f"down3{n}"], 3, -1)

    v["up3l"], v["down3l"] = hop(v["up2l"], 3, 1), hop(v["down2l"], 3, -1)
    for n in range(len(PARTS)):
        v[f"up3{n}"] = v["up2e"][:, edges[n] : edges[n + 1]]
        v[f"down3{n}"] = v["down2e"][:, edges[n] : edges[n + 1]]
    third(0)
    v["over_l"], v["over_e"] = jnp.where(low, v["down2l"], v["up2l"]), jnp.where(low, v["down2e"], v["up2e"])
    v["over_lo"], v["over_eo"] = cores(v["over_l"]), cores(v["over_e"])
    keep_a, give_a = over(0)
    v["sum_a"] = keep_a + halves(give_a)
    v["keep_b"], give_b = over(middle)
    v["give_b"] = halves(give_b)
    fence()
    third(1)
    v["last_l"] = chosen(v["up3l"], v["down3l"], v["up1l"], v["down1l"])
    v["last_lo"] = cores(v["last_l"])
    v["keep0"], v["give0"] = last(0)
    v["sum_b"] = v["keep_b"] + v["give_b"]
    fence()
    third(2)
    v["keep1"], v["give1"] = last(1)
    v["sum0"] = v["keep0"] + halves(v["give0"])
    one = jnp.concatenate([v["sum_a"], v["sum_b"]], 1)
    v["far_one"] = send(
        one.astype(jnp.bfloat16), lambda h, k, z, y: (h, 1 - k, z, 1 - y) if k != z % 2 else None
    )
    fence()

    def home_two(value):
        return send(value.astype(jnp.bfloat16), lambda h, k, z, y: (h, 1 - k, z, 1 - y) if k == z % 2 else None)

    keep, give = last(2)
    sums = [v["sum0"], v["keep1"] + halves(v["give1"]), keep + halves(give)]
    pieces = []
    for n, two in enumerate(sums):
        span = slice(edges[n], edges[n + 1])
        far_two = home_two(two)
        pieces.append((jnp.where(ours, one[:, span], two), jnp.where(ours, v["far_one"][:, span], far_two).astype(jnp.float32)))
    even = [jnp.where(side == 0, a, b) for a, b in pieces]
    odd = [jnp.where(side == 0, b, a) for a, b in pieces]
    return jnp.concatenate(even + odd, 1)


def solution(mesh):
    fits = mesh.shape["arc"] == SPOTS and mesh.shape["col"] == 2 * SPOTS
    return jax.shard_map(
        line_body if fits else gathered_body,
        mesh=mesh,
        in_specs=(P("arc", None, "col"), P("arc", None), P()),
        out_specs=P("col", "arc"),
        check_vma=False,
    )
```

```python
import functools

import jax
import jax.numpy as jnp
from jax import lax
from jax.experimental import pallas as pl
from jax.experimental.pallas import tpu as pltpu
from jax.sharding import PartitionSpec as P

PARTS = (4, 2, 2)
AXES = ("arc", "col")
SPOTS = 4


def band_weights(coef, arc_ids, epochs_here):
    band = coef.shape[1]
    span = epochs_here + band
    start = lax.axis_index("arc") * epochs_here
    ids_all = jnp.concatenate([jnp.full((band,), -1, jnp.int32), arc_ids])
    ids_win = lax.dynamic_slice_in_dim(ids_all, start, span, 0)
    ids_row = lax.dynamic_slice_in_dim(arc_ids, start, epochs_here, 0)
    leading = jnp.concatenate([coef[:, ::-1], jnp.ones((epochs_here, 1), coef.dtype)], 1)
    padded = jnp.concatenate([leading, jnp.zeros((epochs_here, span - band), coef.dtype)], 1)
    skewed = padded.reshape(-1)[: epochs_here * span].reshape(epochs_here, span)
    return jnp.where(ids_row[:, None] == ids_win[None, :], skewed, jnp.zeros_like(skewed))


def window_of(partials, band):
    arcs = lax.axis_size("arc")
    behind = lax.ppermute(partials[partials.shape[0] - band :], "arc", [(a, a + 1) for a in range(arcs - 1)])
    return jnp.concatenate([behind, partials], 0)


def gathered_body(partials, coef, arc_ids):
    epochs_here, channels, width = partials.shape
    weight = band_weights(coef, arc_ids, epochs_here)
    window = window_of(partials, coef.shape[1])
    filtered = jnp.einsum("et,tcm->cem", weight, window, preferred_element_type=jnp.float32)
    filtered = filtered.astype(jnp.bfloat16).reshape(channels * epochs_here, width)
    term = lax.dot_general(
        filtered,
        lax.all_gather(filtered, "col", axis=1, tiled=True),
        (((0,), (0,)), ((), ())),
        preferred_element_type=jnp.float32,
    )
    return lax.psum_scatter(term, "arc", scatter_dimension=1, tiled=True)


def filter_kernel(weight, behind, here, straight, turned):
    band = behind.shape[1]
    found = jnp.dot(weight[:, :band], behind[0], preferred_element_type=jnp.float32)
    found += jnp.dot(weight[:, band:], here[0], preferred_element_type=jnp.float32)
    found = found.astype(jnp.bfloat16)
    straight[...] = found
    turned[...] = found.T


def filter_rows(weight, behind, here):
    channels, count, width = here.shape
    band = behind.shape[1]
    return pl.pallas_call(
        filter_kernel,
        out_shape=(
            jax.ShapeDtypeStruct((channels * count, width), jnp.bfloat16),
            jax.ShapeDtypeStruct((width, channels * count), jnp.bfloat16),
        ),
        grid=(channels,),
        in_specs=[
            pl.BlockSpec((count, band + count), lambda c: (0, 0)),
            pl.BlockSpec((1, band, width), lambda c: (c, 0, 0)),
            pl.BlockSpec((1, count, width), lambda c: (c, 0, 0)),
        ],
        out_specs=(pl.BlockSpec((count, width), lambda c: (c, 0)), pl.BlockSpec((width, count), lambda c: (0, c))),
        compiler_params=pltpu.CompilerParams(vmem_limit_bytes=40 << 20),
        cost_estimate=pl.CostEstimate(
            flops=2 * count * (band + count) * width * channels,
            bytes_accessed=2 * channels * width * (band + 3 * count),
            transcendentals=0,
        ),
    )(weight, behind, here)


def product_kernel(flags, *refs):
    near, far, right, outs = refs[:2], refs[2:4], refs[4:6], refs[6:-2]
    left, arrived = refs[-2:]

    @pl.when(pl.program_id(0) == 0)
    def _():
        for value, group in ((0, near), (1, far)):

            @pl.when(flags[0] == value)
            def _():
                copies = [pltpu.make_async_copy(ref, left.at[i], arrived.at[i]) for i, ref in enumerate(group)]
                for copy in copies:
                    copy.start()
                for copy in copies:
                    copy.wait()

    total = jnp.dot(left[0], right[0][...], preferred_element_type=jnp.float32)
    total += jnp.dot(left[1], right[1][...], preferred_element_type=jnp.float32)
    if len(outs) == 1:
        outs[0][...] = total
    else:
        first, keep, give = outs
        swap = flags[1] == 1
        keep[...] = jnp.where(swap, total, first[...])
        give[...] = jnp.where(swap, first[...], total).astype(give.dtype)


def products(flags, near, far, right, start=0, part=None, first=None):
    rows, depth = near[0].shape
    width = rows
    part = part or width
    tile = min(256, part)

    def spec(height, value):
        shift = start // tile if value.shape[1] == width else 0
        return pl.BlockSpec((height, tile), lambda i, w: (0, shift + i))

    here = pl.BlockSpec((rows, tile), lambda i, w: (0, i))
    whole = jax.ShapeDtypeStruct((rows, part), jnp.float32)
    return pl.pallas_call(
        product_kernel,
        out_shape=whole if first is None else (whole, jax.ShapeDtypeStruct((rows, part), jnp.bfloat16)),
        grid_spec=pltpu.PrefetchScalarGridSpec(
            num_scalar_prefetch=1,
            grid=(part // tile,),
            in_specs=[pl.BlockSpec(memory_space=pl.ANY)] * 4
            + [spec(depth, value) for value in right]
            + ([] if first is None else [spec(rows, first)]),
            out_specs=here if first is None else (here, here),
            scratch_shapes=[pltpu.VMEM((2, rows, depth), near[0].dtype), pltpu.SemaphoreType.DMA((2,))],
        ),
        compiler_params=pltpu.CompilerParams(vmem_limit_bytes=40 << 20),
        cost_estimate=pl.CostEstimate(flops=depth * part, bytes_accessed=depth * part, transcendentals=0),
    )(flags, *near, *far, *right, *([] if first is None else [first]))


def place_kernel(flags, one, keep, came, far_one, far_two, *refs):
    out = refs[-1]
    ours = flags[1] == 1

    @pl.when(pl.program_id(1) == 0)
    def _():
        out[...] = jnp.where(ours, one[...], keep[...] + came[...].astype(jnp.float32))

    @pl.when(pl.program_id(1) == 1)
    def _():
        out[...] = jnp.where(ours, far_one[...], far_two[...]).astype(jnp.float32)


def place(flags, one, keep, came, far_one, far_two, start, held=()):
    rows, width = one.shape
    part = keep.shape[1]
    tile = min(256, part)
    first, count = start // tile, width // tile

    def wide(n, i, w):
        return 0, first + n

    def narrow(n, i, w):
        return 0, n

    return pl.pallas_call(
        place_kernel,
        out_shape=jax.ShapeDtypeStruct((rows, 2 * width), jnp.float32),
        grid_spec=pltpu.PrefetchScalarGridSpec(
            num_scalar_prefetch=1,
            grid=(part // tile, 2),
            in_specs=[
                pl.BlockSpec((rows, tile), wide),
                pl.BlockSpec((rows, tile), narrow),
                pl.BlockSpec((rows, tile), narrow),
                pl.BlockSpec((rows, tile), wide),
                pl.BlockSpec((rows, tile), narrow),
            ]
            + [pl.BlockSpec(memory_space=pl.ANY)] * len(held),
            out_specs=pl.BlockSpec((rows, tile), lambda n, i, w: (0, (w[0] + i) % 2 * count + first + n)),
        ),
        input_output_aliases={6: 0} if held else {},
        compiler_params=pltpu.CompilerParams(vmem_limit_bytes=40 << 20),
        cost_estimate=pl.CostEstimate(flops=rows * part, bytes_accessed=22 * rows * part, transcendentals=0),
    )(flags, one, keep, came, far_one, far_two, *held)


def pairs(arcs, cols, target):
    found = []
    for half in range(arcs // 2):
        for core in range(2):
            for spot in range(cols // 2):
                for side in range(2):
                    place = target(half, core, spot, side)
                    if place is not None:
                        h, k, z, y = place
                        found.append(((2 * half + core) * cols + 2 * spot + side, (2 * h + k) * cols + 2 * z + y))
    return found


def line_body(partials, coef, arc_ids):
    epochs_here, channels, width = partials.shape
    band = coef.shape[1]
    arcs, cols = lax.axis_size("arc"), lax.axis_size("col")
    arc, col = lax.axis_index("arc"), lax.axis_index("col")
    half, core, spot, side = arc // 2, arc % 2, col // 2, col % 2
    cut = epochs_here - band
    unit = width // sum(PARTS)
    edges = [unit * sum(PARTS[:i]) for i in range(len(PARTS) + 1)]
    middle = width // 2

    def send(value, target):
        return lax.ppermute(value, AXES, pairs(arcs, cols, target))

    def hop(value, hops, step):
        def target(h, k, z, y):
            there, origin = z + step, z - step * (hops - 1)
            return (h, k, there, y) if 0 <= there < SPOTS and 0 <= origin < SPOTS else None

        return send(value, target)

    def cores(value):
        return send(value, lambda h, k, z, y: (h, 1 - k, z, y))

    def sides(value):
        return send(value, lambda h, k, z, y: (h, k, z, 1 - y))

    def halves(value):
        return send(value, lambda h, k, z, y: (1 - h, k, z, y))

    v = {}

    def fence():
        v.update(lax.optimization_barrier(dict(v)))

    ours = core == spot % 2
    flag_one = jnp.stack([jnp.where(ours, 0, 1), jnp.where(spot // 2 == half, 0, 1)]).astype(jnp.int32)
    flag_two = jnp.stack([jnp.where(ours, 1, 0), jnp.where(spot % 2 == half, 0, 1)]).astype(jnp.int32)
    low, even_spot = spot < SPOTS // 2, spot % 2 == 0

    weight = band_weights(coef, arc_ids, epochs_here)
    behind = lax.ppermute(jnp.swapaxes(partials[cut:], 0, 1), "arc", [(a, a + 1) for a in range(arcs - 1)])
    v["own"], v["own_t"] = filter_rows(weight, behind, jnp.swapaxes(partials, 0, 1))
    v["up1"], v["down1"] = hop(v["own"], 1, 1), hop(v["own"], 1, -1)
    v["far_t"] = sides(v["own_t"])
    v["own_o"], v["own_to"] = cores(v["own"]), cores(v["own_t"])
    fence()

    def product(flags, *rest):
        return products(flags, [v["own_t"], v["own_to"]], [v["far_t"], v["far_to"]], *rest)

    v["up2"], v["down2"] = hop(v["up1"], 2, 1), hop(v["down1"], 2, -1)
    v["far_to"] = cores(v["far_t"])
    v["sum_own"] = product(flag_one, [v["own"], v["own_o"]])
    v["next"] = jnp.where(low, v["down1"], v["up1"])
    v["next_o"] = cores(v["next"])
    v["sum_next"] = product(flag_two, [v["next"], v["next_o"]])
    fence()

    def over(start):
        return product(flag_one, [v["over"], v["over_o"]], start, middle, v["sum_own"])

    def third(n):
        v[f"up3{n}"], v[f"down3{n}"] = hop(v[f"up3{n}"], 3, 1), hop(v[f"down3{n}"], 3, -1)

    def last(n):
        a, b = edges[n], edges[n + 1]
        stay = jnp.where(even_spot, v["down1"][:, a:b], v["up1"][:, a:b])
        came = jnp.where(spot == 0, v[f"down3{n}"], v[f"up3{n}"])
        block = jnp.where((spot == 0) | (spot == SPOTS - 1), came, stay)
        return product(flag_two, [block, cores(block)], a, b - a, v["sum_next"])

    for n in range(len(PARTS)):
        v[f"up3{n}"] = v["up2"][:, edges[n] : edges[n + 1]]
        v[f"down3{n}"] = v["down2"][:, edges[n] : edges[n + 1]]
    third(0)
    v["over"] = jnp.where(low, v["down2"], v["up2"])
    v["over_o"] = cores(v["over"])
    keep_a, give_a = over(0)
    v["sum_a"] = keep_a + halves(give_a)
    v["keep_b"], v["give_b"] = over(middle)
    fence()
    third(1)
    v["keep0"], v["give0"] = last(0)
    v["give_b"] = halves(v["give_b"])
    fence()
    third(2)
    v["keep1"], v["give1"] = last(1)
    v["give0"] = halves(v["give0"])
    one = jnp.concatenate([v["sum_a"], v["keep_b"] + v["give_b"]], 1)
    v["one"] = one
    v["far_one"] = send(
        one.astype(jnp.bfloat16), lambda h, k, z, y: (h, 1 - k, z, 1 - y) if k != z % 2 else None
    )
    fence()

    def home_two(value):
        return send(value.astype(jnp.bfloat16), lambda h, k, z, y: (h, 1 - k, z, 1 - y) if k == z % 2 else None)

    flags = jnp.stack([side, jnp.where(ours, 1, 0)]).astype(jnp.int32)
    ends = [(v["keep0"], v["give0"]), (v["keep1"], halves(v["give1"]))]
    far_two = [home_two(ends[0][0] + ends[0][1])]
    keep, give = last(2)
    ends.append((keep, halves(give)))
    far_two += [home_two(keep + came) for keep, came in ends[1:]]
    out = ()
    for start, (keep, came), far in zip(edges, ends, far_two):
        out = (place(flags, v["one"], keep, came, v["far_one"], far, start, out),)
    return out[0]


def solution(mesh):
    fits = mesh.shape["arc"] == SPOTS and mesh.shape["col"] == 2 * SPOTS
    return jax.shard_map(
        line_body if fits else gathered_body,
        mesh=mesh,
        in_specs=(P("arc", None, "col"), P("arc", None), P()),
        out_specs=P("col", "arc"),
        check_vma=False,
    )
```

```python
import functools

import jax
import jax.numpy as jnp
from jax import lax
from jax.experimental import pallas as pl
from jax.experimental.pallas import tpu as pltpu
from jax.sharding import PartitionSpec as P

PARTS = (4, 2, 2)
AXES = ("arc", "col")
SPOTS = 4


def band_weights(coef, arc_ids, epochs_here):
    band = coef.shape[1]
    span = epochs_here + band
    start = lax.axis_index("arc") * epochs_here
    ids_all = jnp.concatenate([jnp.full((band,), -1, jnp.int32), arc_ids])
    ids_win = lax.dynamic_slice_in_dim(ids_all, start, span, 0)
    ids_row = lax.dynamic_slice_in_dim(arc_ids, start, epochs_here, 0)
    leading = jnp.concatenate([coef[:, ::-1], jnp.ones((epochs_here, 1), coef.dtype)], 1)
    padded = jnp.concatenate([leading, jnp.zeros((epochs_here, span - band), coef.dtype)], 1)
    skewed = padded.reshape(-1)[: epochs_here * span].reshape(epochs_here, span)
    return jnp.where(ids_row[:, None] == ids_win[None, :], skewed, jnp.zeros_like(skewed))


def window_of(partials, band):
    arcs = lax.axis_size("arc")
    behind = lax.ppermute(partials[partials.shape[0] - band :], "arc", [(a, a + 1) for a in range(arcs - 1)])
    return jnp.concatenate([behind, partials], 0)


def gathered_body(partials, coef, arc_ids):
    epochs_here, channels, width = partials.shape
    weight = band_weights(coef, arc_ids, epochs_here)
    window = window_of(partials, coef.shape[1])
    filtered = jnp.einsum("et,tcm->cem", weight, window, preferred_element_type=jnp.float32)
    filtered = filtered.astype(jnp.bfloat16).reshape(channels * epochs_here, width)
    term = lax.dot_general(
        filtered,
        lax.all_gather(filtered, "col", axis=1, tiled=True),
        (((0,), (0,)), ((), ())),
        preferred_element_type=jnp.float32,
    )
    return lax.psum_scatter(term, "arc", scatter_dimension=1, tiled=True)


def filter_kernel(weight, taken, *refs):
    rows, turned = refs[-2:]
    found = jnp.dot(weight[...], taken[0], preferred_element_type=jnp.float32).astype(jnp.bfloat16)
    rows[...] = found
    turned[...] = found.T


def filter_half(weight, taken, place, held=()):
    channels, lags, width = taken.shape
    count = weight.shape[0]
    half = channels * count
    return pl.pallas_call(
        filter_kernel,
        out_shape=(
            jax.ShapeDtypeStruct((2 * half, width), jnp.bfloat16),
            jax.ShapeDtypeStruct((width, 2 * half), jnp.bfloat16),
        ),
        grid=(channels,),
        in_specs=[
            pl.BlockSpec((count, lags), lambda c: (0, 0)),
            pl.BlockSpec((1, lags, width), lambda c: (c, 0, 0)),
        ]
        + [pl.BlockSpec(memory_space=pl.ANY)] * len(held),
        out_specs=(
            pl.BlockSpec((count, width), lambda c: (place * channels + c, 0)),
            pl.BlockSpec((width, count), lambda c: (0, place * channels + c)),
        ),
        input_output_aliases={2 + i: i for i in range(len(held))},
        compiler_params=pltpu.CompilerParams(vmem_limit_bytes=40 << 20),
        cost_estimate=pl.CostEstimate(
            flops=2 * count * lags * width * channels,
            bytes_accessed=2 * channels * width * (lags + 2 * count),
            transcendentals=0,
        ),
    )(weight, taken, *held)


def cut_kernel(flags, up, down, over, *pieces):
    over[...] = jnp.where(flags[0] == 1, down[...], up[...])
    count = len(pieces) // 2
    for source, group in ((up, pieces[:count]), (down, pieces[count:])):
        start = 0
        for piece in group:
            part = piece.shape[1]
            piece[...] = source[:, start : start + part]
            start += part


def cut_out(from_above, up, down, parts):
    rows, width = up.shape
    tall = rows // 4

    def spec(part):
        return pl.BlockSpec((tall, part), lambda i, w: (i, 0))

    found = pl.pallas_call(
        cut_kernel,
        out_shape=[jax.ShapeDtypeStruct((rows, part), up.dtype) for part in (width, *parts, *parts)],
        grid_spec=pltpu.PrefetchScalarGridSpec(
            num_scalar_prefetch=1,
            grid=(rows // tall,),
            in_specs=[spec(width)] * 2,
            out_specs=[spec(part) for part in (width, *parts, *parts)],
        ),
        compiler_params=pltpu.CompilerParams(vmem_limit_bytes=40 << 20),
        cost_estimate=pl.CostEstimate(flops=rows, bytes_accessed=10 * rows * width, transcendentals=0),
    )(from_above, up, down)
    return found[0], found[1 : 1 + len(parts)], found[1 + len(parts) :]


def product_kernel(flags, *refs):
    near, far, right, outs = refs[:2], refs[2:4], refs[4:6], refs[6:-2]
    left, arrived = refs[-2:]

    @pl.when(pl.program_id(0) == 0)
    def _():
        for value, group in ((0, near), (1, far)):

            @pl.when(flags[0] == value)
            def _():
                copies = [pltpu.make_async_copy(ref, left.at[i], arrived.at[i]) for i, ref in enumerate(group)]
                for copy in copies:
                    copy.start()
                for copy in copies:
                    copy.wait()

    total = jnp.dot(left[0], right[0][...], preferred_element_type=jnp.float32)
    total += jnp.dot(left[1], right[1][...], preferred_element_type=jnp.float32)
    if len(outs) == 1:
        outs[0][...] = total
    else:
        first, keep, give = outs
        swap = flags[1] == 1
        keep[...] = jnp.where(swap, total, first[...])
        give[...] = jnp.where(swap, first[...], total).astype(give.dtype)


def products(flags, near, far, right, start=0, part=None, first=None):
    rows, depth = near[0].shape
    width = rows
    part = part or width
    tile = min(256, part)

    def spec(height, value):
        shift = start // tile if value.shape[1] == width else 0
        return pl.BlockSpec((height, tile), lambda i, w: (0, shift + i))

    here = pl.BlockSpec((rows, tile), lambda i, w: (0, i))
    whole = jax.ShapeDtypeStruct((rows, part), jnp.float32)
    return pl.pallas_call(
        product_kernel,
        out_shape=whole if first is None else (whole, jax.ShapeDtypeStruct((rows, part), jnp.bfloat16)),
        grid_spec=pltpu.PrefetchScalarGridSpec(
            num_scalar_prefetch=1,
            grid=(part // tile,),
            in_specs=[pl.BlockSpec(memory_space=pl.ANY)] * 4
            + [spec(depth, value) for value in right]
            + ([] if first is None else [spec(rows, first)]),
            out_specs=here if first is None else (here, here),
            scratch_shapes=[pltpu.VMEM((2, rows, depth), near[0].dtype), pltpu.SemaphoreType.DMA((2,))],
        ),
        compiler_params=pltpu.CompilerParams(vmem_limit_bytes=40 << 20),
        cost_estimate=pl.CostEstimate(flops=depth * part, bytes_accessed=depth * part, transcendentals=0),
    )(flags, *near, *far, *right, *([] if first is None else [first]))


def place_kernel(flags, one, keep, came, far_one, far_two, *refs):
    out = refs[-1]
    ours = flags[1] == 1

    @pl.when(pl.program_id(1) == 0)
    def _():
        out[...] = jnp.where(ours, one[...], keep[...] + came[...].astype(jnp.float32))

    @pl.when(pl.program_id(1) == 1)
    def _():
        out[...] = jnp.where(ours, far_one[...], far_two[...]).astype(jnp.float32)


def place(flags, one, keep, came, far_one, far_two, start, held=()):
    rows, width = one.shape
    part = keep.shape[1]
    tile = min(256, part)
    first, count = start // tile, width // tile

    def wide(n, i, w):
        return 0, first + n

    def narrow(n, i, w):
        return 0, n

    return pl.pallas_call(
        place_kernel,
        out_shape=jax.ShapeDtypeStruct((rows, 2 * width), jnp.float32),
        grid_spec=pltpu.PrefetchScalarGridSpec(
            num_scalar_prefetch=1,
            grid=(part // tile, 2),
            in_specs=[
                pl.BlockSpec((rows, tile), wide),
                pl.BlockSpec((rows, tile), narrow),
                pl.BlockSpec((rows, tile), narrow),
                pl.BlockSpec((rows, tile), wide),
                pl.BlockSpec((rows, tile), narrow),
            ]
            + [pl.BlockSpec(memory_space=pl.ANY)] * len(held),
            out_specs=pl.BlockSpec((rows, tile), lambda n, i, w: (0, (w[0] + i) % 2 * count + first + n)),
        ),
        input_output_aliases={6: 0} if held else {},
        compiler_params=pltpu.CompilerParams(vmem_limit_bytes=40 << 20),
        cost_estimate=pl.CostEstimate(flops=rows * part, bytes_accessed=22 * rows * part, transcendentals=0),
    )(flags, one, keep, came, far_one, far_two, *held)


def pairs(arcs, cols, target):
    found = []
    for half in range(arcs // 2):
        for core in range(2):
            for spot in range(cols // 2):
                for side in range(2):
                    place = target(half, core, spot, side)
                    if place is not None:
                        h, k, z, y = place
                        found.append(((2 * half + core) * cols + 2 * spot + side, (2 * h + k) * cols + 2 * z + y))
    return found


def line_body(partials, coef, arc_ids):
    epochs_here, channels, width = partials.shape
    band = coef.shape[1]
    arcs, cols = lax.axis_size("arc"), lax.axis_size("col")
    arc, col = lax.axis_index("arc"), lax.axis_index("col")
    half, core, spot, side = arc // 2, arc % 2, col // 2, col % 2
    cut = epochs_here - band
    unit = width // sum(PARTS)
    edges = [unit * sum(PARTS[:i]) for i in range(len(PARTS) + 1)]
    middle = width // 2

    def send(value, target):
        return lax.ppermute(value, AXES, pairs(arcs, cols, target))

    def hop(value, hops, step):
        def target(h, k, z, y):
            there, origin = z + step, z - step * (hops - 1)
            return (h, k, there, y) if 0 <= there < SPOTS and 0 <= origin < SPOTS else None

        return send(value, target)

    def cores(value):
        return send(value, lambda h, k, z, y: (h, 1 - k, z, y))

    def sides(value):
        return send(value, lambda h, k, z, y: (h, k, z, 1 - y))

    def halves(value):
        return send(value, lambda h, k, z, y: (1 - h, k, z, y))

    v = {}

    def fence():
        v.update(lax.optimization_barrier(dict(v)))

    ours = core == spot % 2
    flag_one = jnp.stack([jnp.where(ours, 0, 1), jnp.where(spot // 2 == half, 0, 1)]).astype(jnp.int32)
    flag_two = jnp.stack([jnp.where(ours, 1, 0), jnp.where(spot % 2 == half, 0, 1)]).astype(jnp.int32)
    low, even_spot = spot < SPOTS // 2, spot % 2 == 0

    weight = band_weights(coef, arc_ids, epochs_here)
    behind = lax.ppermute(partials[cut:], "arc", [(a, a + 1) for a in range(arcs - 1)])
    here = jnp.swapaxes(partials, 0, 1)
    held = filter_half(weight[band:, band:], here, 0)
    first = jnp.concatenate([jnp.swapaxes(behind, 0, 1), here[:, :band]], 1)
    v["own"], v["own_t"] = filter_half(weight[:band, : 2 * band], first, 1, held)
    v["up1"], v["down1"] = hop(v["own"], 1, 1), hop(v["own"], 1, -1)
    v["far_t"] = sides(v["own_t"])
    v["own_o"], v["own_to"] = cores(v["own"]), cores(v["own_t"])
    fence()

    def product(flags, *rest):
        return products(flags, [v["own_t"], v["own_to"]], [v["far_t"], v["far_to"]], *rest)

    v["up2"], v["down2"] = hop(v["up1"], 2, 1), hop(v["down1"], 2, -1)
    v["far_to"] = cores(v["far_t"])
    v["sum_own"] = product(flag_one, [v["own"], v["own_o"]])
    v["next"] = jnp.where(low, v["down1"], v["up1"])
    v["next_o"] = cores(v["next"])
    v["sum_next"] = product(flag_two, [v["next"], v["next_o"]])
    fence()

    def over(start):
        return product(flag_one, [v["over"], v["over_o"]], start, middle, v["sum_own"])

    def third(n):
        v[f"up3{n}"], v[f"down3{n}"] = hop(v[f"up3{n}"], 3, 1), hop(v[f"down3{n}"], 3, -1)

    def last(n):
        a, b = edges[n], edges[n + 1]
        stay = jnp.where(even_spot, v["down1"][:, a:b], v["up1"][:, a:b])
        came = jnp.where(spot == 0, v[f"down3{n}"], v[f"up3{n}"])
        block = jnp.where((spot == 0) | (spot == SPOTS - 1), came, stay)
        return product(flag_two, [block, cores(block)], a, b - a, v["sum_next"])

    for n in range(len(PARTS)):
        v[f"up3{n}"] = v["up2"][:, edges[n] : edges[n + 1]]
        v[f"down3{n}"] = v["down2"][:, edges[n] : edges[n + 1]]
    third(0)
    v["over"] = jnp.where(low, v["down2"], v["up2"])
    v["over_o"] = cores(v["over"])
    keep_a, give_a = over(0)
    v["sum_a"] = keep_a + halves(give_a)
    v["keep_b"], v["give_b"] = over(middle)
    fence()
    third(1)
    v["keep0"], v["give0"] = last(0)
    v["give_b"] = halves(v["give_b"])
    fence()
    third(2)
    v["keep1"], v["give1"] = last(1)
    v["give0"] = halves(v["give0"])
    one = jnp.concatenate([v["sum_a"], v["keep_b"] + v["give_b"]], 1)
    v["one"] = one
    v["far_one"] = send(
        one.astype(jnp.bfloat16), lambda h, k, z, y: (h, 1 - k, z, 1 - y) if k != z % 2 else None
    )
    fence()

    def home_two(value):
        return send(value.astype(jnp.bfloat16), lambda h, k, z, y: (h, 1 - k, z, 1 - y) if k == z % 2 else None)

    flags = jnp.stack([side, jnp.where(ours, 1, 0)]).astype(jnp.int32)
    ends = [(v["keep0"], v["give0"]), (v["keep1"], halves(v["give1"]))]
    far_two = [home_two(ends[0][0] + ends[0][1])]
    keep, give = last(2)
    ends.append((keep, halves(give)))
    far_two += [home_two(keep + came) for keep, came in ends[1:]]
    out = ()
    for start, (keep, came), far in zip(edges, ends, far_two):
        out = (place(flags, v["one"], keep, came, v["far_one"], far, start, out),)
    return out[0]


def solution(mesh):
    fits = mesh.shape["arc"] == SPOTS and mesh.shape["col"] == 2 * SPOTS
    return jax.shard_map(
        line_body if fits else gathered_body,
        mesh=mesh,
        in_specs=(P("arc", None, "col"), P("arc", None), P()),
        out_specs=P("col", "arc"),
        check_vma=False,
    )
```

```python
import functools

import jax
import jax.numpy as jnp
from jax import lax
from jax.experimental import pallas as pl
from jax.experimental.pallas import tpu as pltpu
from jax.sharding import PartitionSpec as P

PARTS = (4, 2, 2)
AXES = ("arc", "col")
SPOTS = 4


def band_weights(coef, arc_ids, epochs_here):
    band = coef.shape[1]
    span = epochs_here + band
    start = lax.axis_index("arc") * epochs_here
    ids_all = jnp.concatenate([jnp.full((band,), -1, jnp.int32), arc_ids])
    ids_win = lax.dynamic_slice_in_dim(ids_all, start, span, 0)
    ids_row = lax.dynamic_slice_in_dim(arc_ids, start, epochs_here, 0)
    leading = jnp.concatenate([coef[:, ::-1], jnp.ones((epochs_here, 1), coef.dtype)], 1)
    padded = jnp.concatenate([leading, jnp.zeros((epochs_here, span - band), coef.dtype)], 1)
    skewed = padded.reshape(-1)[: epochs_here * span].reshape(epochs_here, span)
    return jnp.where(ids_row[:, None] == ids_win[None, :], skewed, jnp.zeros_like(skewed))


def window_of(partials, band):
    arcs = lax.axis_size("arc")
    behind = lax.ppermute(partials[partials.shape[0] - band :], "arc", [(a, a + 1) for a in range(arcs - 1)])
    return jnp.concatenate([behind, partials], 0)


def gathered_body(partials, coef, arc_ids):
    epochs_here, channels, width = partials.shape
    weight = band_weights(coef, arc_ids, epochs_here)
    window = window_of(partials, coef.shape[1])
    filtered = jnp.einsum("et,tcm->cem", weight, window, preferred_element_type=jnp.float32)
    filtered = filtered.astype(jnp.bfloat16).reshape(channels * epochs_here, width)
    term = lax.dot_general(
        filtered,
        lax.all_gather(filtered, "col", axis=1, tiled=True),
        (((0,), (0,)), ((), ())),
        preferred_element_type=jnp.float32,
    )
    return lax.psum_scatter(term, "arc", scatter_dimension=1, tiled=True)


def filter_kernel(weight, taken, *refs):
    rows, turned = refs[-2:]
    found = jnp.dot(weight[...], taken[0], preferred_element_type=jnp.float32).astype(jnp.bfloat16)
    rows[...] = found
    turned[...] = found.T


def filter_half(weight, taken, place, held=()):
    channels, lags, width = taken.shape
    count = weight.shape[0]
    half = channels * count
    return pl.pallas_call(
        filter_kernel,
        out_shape=(
            jax.ShapeDtypeStruct((2 * half, width), jnp.bfloat16),
            jax.ShapeDtypeStruct((width, 2 * half), jnp.bfloat16),
        ),
        grid=(channels,),
        in_specs=[
            pl.BlockSpec((count, lags), lambda c: (0, 0)),
            pl.BlockSpec((1, lags, width), lambda c: (c, 0, 0)),
        ]
        + [pl.BlockSpec(memory_space=pl.ANY)] * len(held),
        out_specs=(
            pl.BlockSpec((count, width), lambda c: (place * channels + c, 0)),
            pl.BlockSpec((width, count), lambda c: (0, place * channels + c)),
        ),
        input_output_aliases={2 + i: i for i in range(len(held))},
        compiler_params=pltpu.CompilerParams(vmem_limit_bytes=24 << 20),
        cost_estimate=pl.CostEstimate(
            flops=2 * count * lags * width * channels,
            bytes_accessed=2 * channels * width * (lags + 2 * count),
            transcendentals=0,
        ),
    )(weight, taken, *held)


def cut_kernel(flags, up, down, over, *pieces):
    over[...] = jnp.where(flags[0] == 1, down[...], up[...])
    count = len(pieces) // 2
    for source, group in ((up, pieces[:count]), (down, pieces[count:])):
        start = 0
        for piece in group:
            part = piece.shape[1]
            piece[...] = source[:, start : start + part]
            start += part


def cut_out(from_above, up, down, parts):
    rows, width = up.shape
    tall = rows // 4

    def spec(part):
        return pl.BlockSpec((tall, part), lambda i, w: (i, 0))

    found = pl.pallas_call(
        cut_kernel,
        out_shape=[jax.ShapeDtypeStruct((rows, part), up.dtype) for part in (width, *parts, *parts)],
        grid_spec=pltpu.PrefetchScalarGridSpec(
            num_scalar_prefetch=1,
            grid=(rows // tall,),
            in_specs=[spec(width)] * 2,
            out_specs=[spec(part) for part in (width, *parts, *parts)],
        ),
        compiler_params=pltpu.CompilerParams(vmem_limit_bytes=24 << 20),
        cost_estimate=pl.CostEstimate(flops=rows, bytes_accessed=10 * rows * width, transcendentals=0),
    )(from_above, up, down)
    return found[0], found[1 : 1 + len(parts)], found[1 + len(parts) :]


def product_kernel(flags, *refs):
    near, far, right, outs = refs[:2], refs[2:4], refs[4:6], refs[6:-2]
    left, arrived = refs[-2:]

    @pl.when(pl.program_id(0) == 0)
    def _():
        for value, group in ((0, near), (1, far)):

            @pl.when(flags[0] == value)
            def _():
                copies = [pltpu.make_async_copy(ref, left.at[i], arrived.at[i]) for i, ref in enumerate(group)]
                for copy in copies:
                    copy.start()
                for copy in copies:
                    copy.wait()

    total = jnp.dot(left[0], right[0][...], preferred_element_type=jnp.float32)
    total += jnp.dot(left[1], right[1][...], preferred_element_type=jnp.float32)
    if len(outs) == 1:
        outs[0][...] = total
    else:
        first, keep, give = outs
        swap = flags[1] == 1
        keep[...] = jnp.where(swap, total, first[...])
        give[...] = jnp.where(swap, first[...], total).astype(give.dtype)


def products(flags, near, far, right, start=0, part=None, first=None):
    rows, depth = near[0].shape
    width = rows
    part = part or width
    tile = min(256, part)

    def spec(height, value):
        shift = start // tile if value.shape[1] == width else 0
        return pl.BlockSpec((height, tile), lambda i, w: (0, shift + i))

    here = pl.BlockSpec((rows, tile), lambda i, w: (0, i))
    whole = jax.ShapeDtypeStruct((rows, part), jnp.float32)
    return pl.pallas_call(
        product_kernel,
        out_shape=whole if first is None else (whole, jax.ShapeDtypeStruct((rows, part), jnp.bfloat16)),
        grid_spec=pltpu.PrefetchScalarGridSpec(
            num_scalar_prefetch=1,
            grid=(part // tile,),
            in_specs=[pl.BlockSpec(memory_space=pl.ANY)] * 4
            + [spec(depth, value) for value in right]
            + ([] if first is None else [spec(rows, first)]),
            out_specs=here if first is None else (here, here),
            scratch_shapes=[pltpu.VMEM((2, rows, depth), near[0].dtype), pltpu.SemaphoreType.DMA((2,))],
        ),
        compiler_params=pltpu.CompilerParams(vmem_limit_bytes=24 << 20),
        cost_estimate=pl.CostEstimate(flops=depth * part, bytes_accessed=depth * part, transcendentals=0),
    )(flags, *near, *far, *right, *([] if first is None else [first]))


def place_kernel(flags, one, keep, came, far_one, far_two, *refs):
    out = refs[-1]
    ours = flags[1] == 1

    @pl.when(pl.program_id(1) == 0)
    def _():
        out[...] = jnp.where(ours, one[...], keep[...] + came[...].astype(jnp.float32))

    @pl.when(pl.program_id(1) == 1)
    def _():
        out[...] = jnp.where(ours, far_one[...], far_two[...]).astype(jnp.float32)


def place(flags, one, keep, came, far_one, far_two, start, held=()):
    rows, width = one.shape
    part = keep.shape[1]
    tile = min(256, part)
    first, count = start // tile, width // tile

    def wide(n, i, w):
        return 0, first + n

    def narrow(n, i, w):
        return 0, n

    return pl.pallas_call(
        place_kernel,
        out_shape=jax.ShapeDtypeStruct((rows, 2 * width), jnp.float32),
        grid_spec=pltpu.PrefetchScalarGridSpec(
            num_scalar_prefetch=1,
            grid=(part // tile, 2),
            in_specs=[
                pl.BlockSpec((rows, tile), wide),
                pl.BlockSpec((rows, tile), narrow),
                pl.BlockSpec((rows, tile), narrow),
                pl.BlockSpec((rows, tile), wide),
                pl.BlockSpec((rows, tile), narrow),
            ]
            + [pl.BlockSpec(memory_space=pl.ANY)] * len(held),
            out_specs=pl.BlockSpec((rows, tile), lambda n, i, w: (0, (w[0] + i) % 2 * count + first + n)),
        ),
        input_output_aliases={6: 0} if held else {},
        compiler_params=pltpu.CompilerParams(vmem_limit_bytes=24 << 20),
        cost_estimate=pl.CostEstimate(flops=rows * part, bytes_accessed=22 * rows * part, transcendentals=0),
    )(flags, one, keep, came, far_one, far_two, *held)


def pairs(arcs, cols, target):
    found = []
    for half in range(arcs // 2):
        for core in range(2):
            for spot in range(cols // 2):
                for side in range(2):
                    place = target(half, core, spot, side)
                    if place is not None:
                        h, k, z, y = place
                        found.append(((2 * half + core) * cols + 2 * spot + side, (2 * h + k) * cols + 2 * z + y))
    return found


def line_body(partials, coef, arc_ids):
    epochs_here, channels, width = partials.shape
    band = coef.shape[1]
    arcs, cols = lax.axis_size("arc"), lax.axis_size("col")
    arc, col = lax.axis_index("arc"), lax.axis_index("col")
    half, core, spot, side = arc // 2, arc % 2, col // 2, col % 2
    cut = epochs_here - band
    unit = width // sum(PARTS)
    edges = [unit * sum(PARTS[:i]) for i in range(len(PARTS) + 1)]
    middle = width // 2

    def send(value, target):
        return lax.ppermute(value, AXES, pairs(arcs, cols, target))

    def hop(value, hops, step):
        def target(h, k, z, y):
            there, origin = z + step, z - step * (hops - 1)
            return (h, k, there, y) if 0 <= there < SPOTS and 0 <= origin < SPOTS else None

        return send(value, target)

    def cores(value):
        return send(value, lambda h, k, z, y: (h, 1 - k, z, y))

    def sides(value):
        return send(value, lambda h, k, z, y: (h, k, z, 1 - y))

    def halves(value):
        return send(value, lambda h, k, z, y: (1 - h, k, z, y))

    v = {}

    def fence():
        v.update(lax.optimization_barrier(dict(v)))

    ours = core == spot % 2
    flag_one = jnp.stack([jnp.where(ours, 0, 1), jnp.where(spot // 2 == half, 0, 1)]).astype(jnp.int32)
    flag_two = jnp.stack([jnp.where(ours, 1, 0), jnp.where(spot % 2 == half, 0, 1)]).astype(jnp.int32)
    low, even_spot = spot < SPOTS // 2, spot % 2 == 0

    weight = band_weights(coef, arc_ids, epochs_here)
    behind = lax.ppermute(partials[cut:], "arc", [(a, a + 1) for a in range(arcs - 1)])
    here = jnp.swapaxes(partials, 0, 1)
    held = filter_half(weight[band:, band:], here, 0)
    first = jnp.concatenate([jnp.swapaxes(behind, 0, 1), here[:, :band]], 1)
    v["own"], v["own_t"] = filter_half(weight[:band, : 2 * band], first, 1, held)
    v["up1"], v["down1"] = hop(v["own"], 1, 1), hop(v["own"], 1, -1)
    v["far_t"] = sides(v["own_t"])
    v["own_o"], v["own_to"] = cores(v["own"]), cores(v["own_t"])
    fence()

    def product(flags, *rest):
        return products(flags, [v["own_t"], v["own_to"]], [v["far_t"], v["far_to"]], *rest)

    v["up2"], v["down2"] = hop(v["up1"], 2, 1), hop(v["down1"], 2, -1)
    v["far_to"] = cores(v["far_t"])
    v["sum_own"] = product(flag_one, [v["own"], v["own_o"]])
    v["next"] = jnp.where(low, v["down1"], v["up1"])
    v["next_o"] = cores(v["next"])
    v["sum_next"] = product(flag_two, [v["next"], v["next_o"]])
    fence()

    def over(start):
        return product(flag_one, [v["over"], v["over_o"]], start, middle, v["sum_own"])

    def third(n):
        v[f"up3{n}"], v[f"down3{n}"] = hop(v[f"up3{n}"], 3, 1), hop(v[f"down3{n}"], 3, -1)

    def last(n):
        a, b = edges[n], edges[n + 1]
        stay = jnp.where(even_spot, v["down1"][:, a:b], v["up1"][:, a:b])
        came = jnp.where(spot == 0, v[f"down3{n}"], v[f"up3{n}"])
        block = jnp.where((spot == 0) | (spot == SPOTS - 1), came, stay)
        return product(flag_two, [block, cores(block)], a, b - a, v["sum_next"])

    for n in range(len(PARTS)):
        v[f"up3{n}"] = v["up2"][:, edges[n] : edges[n + 1]]
        v[f"down3{n}"] = v["down2"][:, edges[n] : edges[n + 1]]
    third(0)
    v["over"] = jnp.where(low, v["down2"], v["up2"])
    v["over_o"] = cores(v["over"])
    keep_a, give_a = over(0)
    v["sum_a"] = keep_a + halves(give_a)
    v["keep_b"], v["give_b"] = over(middle)
    fence()
    third(1)
    v["keep0"], v["give0"] = last(0)
    v["give_b"] = halves(v["give_b"])
    fence()
    third(2)
    v["keep1"], v["give1"] = last(1)
    v["give0"] = halves(v["give0"])
    one = jnp.concatenate([v["sum_a"], v["keep_b"] + v["give_b"]], 1)
    v["one"] = one
    v["far_one"] = send(
        one.astype(jnp.bfloat16), lambda h, k, z, y: (h, 1 - k, z, 1 - y) if k != z % 2 else None
    )
    fence()

    def home_two(value):
        return send(value.astype(jnp.bfloat16), lambda h, k, z, y: (h, 1 - k, z, 1 - y) if k == z % 2 else None)

    flags = jnp.stack([side, jnp.where(ours, 1, 0)]).astype(jnp.int32)
    ends = [(v["keep0"], v["give0"]), (v["keep1"], halves(v["give1"]))]
    far_two = [home_two(ends[0][0] + ends[0][1])]
    keep, give = last(2)
    ends.append((keep, halves(give)))
    far_two += [home_two(keep + came) for keep, came in ends[1:]]
    out = ()
    for start, (keep, came), far in zip(edges, ends, far_two):
        out = (place(flags, v["one"], keep, came, v["far_one"], far, start, out),)
    return out[0]


def solution(mesh):
    fits = mesh.shape["arc"] == SPOTS and mesh.shape["col"] == 2 * SPOTS
    return jax.shard_map(
        line_body if fits else gathered_body,
        mesh=mesh,
        in_specs=(P("arc", None, "col"), P("arc", None), P()),
        out_specs=P("col", "arc"),
        check_vma=False,
    )
```
